32 devices in a mesh: dp: 8 (over y, x, core), tensor: 4 (over z).
Axes of the slice: x: 2, y: 2, z: 4, core: 2. Of those that a mesh axis runs over, the one named last changes fastest.
Arguments:
- tokens: bfloat16 [16384, 768], P('dp'), may hold values from -6 to 6
- w_qkv: bfloat16 [3, 768, 768], P(None, None, 'tensor'), may hold values from -0.21875 to 0.21875
- b_qv: float32 [2, 768], P(None, 'tensor'), may hold values from -3 to 3
- w_out: bfloat16 [768, 768], P('tensor'), may hold values from -1.25 to 1.25
- b_out: float32 [768], replicated, may hold values from -3 to 3
- ln1_gain: float32 [768], replicated, may hold values from 0.25 to 1.75
- ln1_bias: float32 [768], replicated, may hold values from -3 to 3
- w_up: bfloat16 [768, 3072], P(None, 'tensor'), may hold values from -0.21875 to 0.21875
- b_up: float32 [3072], P('tensor'), may hold values from -3 to 3
- w_down: bfloat16 [3072, 768], P('tensor'), may hold values from -0.109375 to 0.109375
- b_down: float32 [768], replicated, may hold values from -3 to 3
- ln2_gain: float32 [768], replicated, may hold values from 0.25 to 1.75
- ln2_bias: float32 [768], replicated, may hold values from -3 to 3
- lengths: int32 [32], P('dp'), may hold values from 128 to 512, as said below
- picks: int32 [32, 128], P('dp'), may hold values from 0 to 512, as said below
- cotangent: float32 [16384, 768], P('dp'), may hold values from -6 to 6
Outputs:
- output: bfloat16 [16384, 768], P('dp')
- grad_tokens: float32 [16384, 768], P('dp')
- grad_w_qkv: float32 [3, 768, 768], P(None, None, 'tensor')
- grad_b_qv: float32 [2, 768], P(None, 'tensor')
- grad_w_out: float32 [768, 768], P('tensor')
- grad_b_out: float32 [768], replicated
- grad_ln1_gain: float32 [768], replicated
- grad_ln1_bias: float32 [768], replicated
- grad_w_up: float32 [768, 3072], P(None, 'tensor')
- grad_b_up: float32 [3072], P('tensor')
- grad_w_down: float32 [3072, 768], P('tensor')
- grad_b_down: float32 [768], replicated
- grad_ln2_gain: float32 [768], replicated
- grad_ln2_bias: float32 [768], replicated
The draws below stay inside these ranges and needn't reach their ends.
Inputs may be any that keep to these rules, and one draw needn't show every extreme that they name: `lengths`: some sequences have the full length 512. `picks`: each row lists distinct positions of its sequence in its first slots and the value 512 in the rest; every row lists at least 16 positions and leaves at least one slot unused.
All inputs are finite; a program needn't handle non-finite values.
Results may differ from the reference program's by a relative error of at most 0.013.
The reference program's roundings to bfloat16 on the way count: a program that leaves them out, or rounds other values in their place, can miss the bound.
Values sent between devices are 32-bit elements; how exact they have to be, the bound alone decides.
A program may use at most 128 MiB of HBM per device.

```python
from functools import partial
import jax
import jax.numpy as jnp
from jax import lax

D = 768
H = 12
HD = 64
FF = 3072
SEQ = 512
PICKS = 128
SEQS = 32
TOKENS = 16384


def draw_lengths(key, part):
    first_key, second_key = jax.random.split(key)
    partial_len = jax.random.randint(first_key, (SEQS,), SEQ // 4, SEQ)
    full_flag = jax.random.randint(second_key, (SEQS,), 0, 4) == 0
    drawn = jnp.where(full_flag, SEQ, partial_len)
    return drawn.at[0].set(SEQ).astype(jnp.int32)


def draw_picks(key, part):
    count_key, order_key = jax.random.split(key)
    counts = jax.random.randint(count_key, (SEQS, 1), PICKS // 8, PICKS)
    row_keys = jax.random.split(order_key, SEQS)
    orders = jax.vmap(lambda row_key: jax.random.permutation(row_key, SEQ)[:PICKS])(row_keys)
    slot_index = jnp.arange(PICKS)[None, :]
    return jnp.where(slot_index < counts, orders, SEQ).astype(jnp.int32)


def level_of(own_key, dims, shards, smallest, high):
    loudness, own = 1.0, jax.random.fold_in(own_key, 6)
    for axis_at, blocks in shards:
        heights = jnp.exp(jax.random.uniform(jax.random.fold_in(own, axis_at), (blocks,), jnp.float32, smallest / len(shards), high / len(shards)))
        loudness = loudness * jnp.repeat(heights, dims[axis_at] // blocks).reshape([-1 if axis == axis_at else 1 for axis in range(len(dims))])
    return loudness


def centred(key, dims, spread, bound, cuts=(), held_as=jnp.bfloat16):
    result = jax.random.normal(key, dims, jnp.float32) * spread
    if len(cuts) > 0:
        result = level_of(key, dims, cuts, -0.22, 0.18) * result
    return jnp.clip(result, min=-bound, max=bound).astype(held_as)


def setup_inputs(seed: int = 0) -> dict:
    splits = jax.random.split(jax.random.key(seed), 17)
    tokens = centred(splits[0], (TOKENS, D), 1.0, 6.0, ((0, 8),))
    w_qkv = centred(splits[1], (3, D, D), D ** -0.5, 0.21875, ((2, 4),))
    b_qv = centred(splits[2], (2, D), 0.5, 3.0, ((1, 4),), jnp.float32)
    w_out = centred(splits[3], (D, D), (D // 32) ** -0.5, 1.25, ((0, 4),))
    b_out = centred(splits[4], (D,), 0.5, 3.0, (), jnp.float32)
    ln1_gain = jnp.clip(1.0 + 0.15 * jax.random.normal(splits[5], (D,), jnp.float32), 0.25, 1.75)
    ln1_bias = centred(splits[6], (D,), 0.5, 3.0, (), jnp.float32)
    w_up = centred(splits[7], (D, FF), D ** -0.5, 0.21875, ((1, 4),))
    b_up = centred(splits[8], (FF,), 0.5, 3.0, ((0, 4),), jnp.float32)
    w_down = centred(splits[9], (FF, D), FF ** -0.5, 0.109375, ((0, 4),))
    b_down = centred(splits[10], (D,), 0.5, 3.0, (), jnp.float32)
    ln2_gain = jnp.clip(1.0 + 0.15 * jax.random.normal(splits[11], (D,), jnp.float32), 0.25, 1.75)
    ln2_bias = centred(splits[12], (D,), 0.5, 3.0, (), jnp.float32)
    lengths = draw_lengths(jax.random.fold_in(splits[16], 71), 0)
    picks = draw_picks(jax.random.fold_in(splits[16], 71), 0)
    cotangent = centred(splits[15], (TOKENS, D), 1.0, 6.0, ((0, 8),), jnp.float32)
    return dict(tokens=tokens, w_qkv=w_qkv, b_qv=b_qv, w_out=w_out, b_out=b_out, ln1_gain=ln1_gain, ln1_bias=ln1_bias, w_up=w_up, b_up=b_up, w_down=w_down, b_down=b_down, ln2_gain=ln2_gain, ln2_bias=ln2_bias, lengths=lengths, picks=picks, cotangent=cotangent)


EPS = 1e-05
SCALE = 0.125
HIGH = lax.Precision.HIGHEST

@jax.custom_vjp
def low(v):
    return lax.optimization_barrier(v.astype(jnp.bfloat16)).astype(jnp.float32)

@jax.custom_vjp
def low_back(v):
    return v

def low_keep(v):
    return (low(v), None)

def low_pass(kept, grad):
    return (grad,)

def back_keep(v):
    return (v, None)

def back_low(kept, grad):
    return (low(grad),)
low.defvjp(low_keep, low_pass)
low_back.defvjp(back_keep, back_low)

def layer_norm(tok_rows, ln_gain, ln_shift):
    centered = tok_rows - lax.optimization_barrier(jnp.mean(tok_rows, axis=-1, keepdims=True))
    variance = lax.optimization_barrier(jnp.mean(centered * centered, axis=-1, keepdims=True))
    return centered * lax.rsqrt(variance + EPS) * ln_gain + ln_shift

def product(left, right):
    return jnp.dot(left, right, precision=HIGH)

def attend(pieces):
    queries, key_rows, values, seq_length = pieces
    scores = jnp.einsum('qhd,khd->hqk', queries, key_rows, precision=HIGH) * SCALE
    scores = low_back(scores)
    is_valid = jnp.arange(SEQ) < seq_length
    scores = jnp.where(is_valid[None, None, :], scores, -1e+30)
    weights = low(jax.nn.softmax(scores, axis=-1))
    return jnp.einsum('hqk,khd->qhd', weights, values, precision=HIGH)

def split_heads(flat_rows):
    return flat_rows.reshape(SEQS, SEQ, H, HD)

def forward(lengths, tokens, w_qkv, b_qv, w_out, b_out, ln1_gain, ln1_bias, w_up, b_up, w_down, b_down, ln2_gain, ln2_bias):
    queries = low(low_back(product(tokens, w_qkv[0]) + b_qv[0]))
    key_rows = low(low_back(product(tokens, w_qkv[1])))
    values = low(low_back(product(tokens, w_qkv[2]) + b_qv[1]))
    attended = lax.map(jax.checkpoint(attend), (split_heads(queries), split_heads(key_rows), split_heads(values), lengths))
    attended = low(low_back(attended.reshape(TOKENS, D)))
    first_sum = tokens + low_back(product(attended, w_out)) + b_out
    normed = layer_norm(first_sum, ln1_gain, ln1_bias)
    ffn_inner = low_back(product(low(normed), w_up) + b_up)
    active = low(jax.nn.gelu(ffn_inner, approximate=False))
    second_sum = normed + low_back(product(active, w_down)) + b_down
    return layer_norm(second_sum, ln2_gain, ln2_bias)

def reference(tokens, w_qkv, b_qv, w_out, b_out, ln1_gain, ln1_bias, w_up, b_up, w_down, b_down, ln2_gain, ln2_bias, lengths, picks, cotangent):
    floats = [array.astype(jnp.float32) for array in (tokens, w_qkv, b_qv, w_out, b_out, ln1_gain, ln1_bias, w_up, b_up, w_down, b_down, ln2_gain, ln2_bias)]
    output, pull = jax.vjp(partial(forward, lengths), *floats)
    keep_mask = jnp.any(picks[:, :, None] == jnp.arange(SEQ)[None, None, :], axis=1)
    grads = pull(cotangent * keep_mask.reshape(TOKENS, 1).astype(jnp.float32))
    return (output.astype(jnp.bfloat16), grads[0], grads[1], grads[2], grads[3], grads[4], grads[5], grads[6], grads[7], grads[8], grads[9], grads[10], grads[11], grads[12])
```

```python
import functools

import jax
import jax.numpy as jnp
from jax import lax
from jax.experimental import pallas as pl
from jax.experimental.pallas import tpu as pltpu
from jax.sharding import PartitionSpec as P

HD = 64
PAIR = 2 * HD
EPS = 1e-05
SCALE = 0.125
NEG = -1e30
F32 = jnp.float32
BF16 = jnp.bfloat16


def dot(a, b, ca, cb):
    return lax.dot_general(a, b, (((ca,), (cb,)), ((), ())), preferred_element_type=F32)


def halves(block):
    lane = lax.broadcasted_iota(jnp.int32, block.shape, 1)
    zero = jnp.zeros_like(block)
    return jnp.concatenate([jnp.where(lane < HD, block, zero), jnp.where(lane < HD, zero, block)], axis=0)


def merge(stacked):
    rows = stacked.shape[0] // 2
    lane = lax.broadcasted_iota(jnp.int32, (rows, PAIR), 1)
    return jnp.where(lane < HD, stacked[:rows], stacked[rows:])


def softmax_rows(stacked_q, keys, length):
    scores = dot(stacked_q * SCALE, keys, 1, 1)
    key_at = lax.broadcasted_iota(jnp.int32, (1, keys.shape[0]), 1)
    scores = scores + jnp.where(key_at < length, 0.0, NEG)
    top = jnp.max(scores, axis=-1, keepdims=True)
    e = jnp.exp(scores - top)
    return e / jnp.sum(e, axis=-1, keepdims=True)


def attend_kernel(first_ref, lengths_ref, q_ref, k_ref, v_ref, o_ref):
    length = lengths_ref[first_ref[0] + pl.program_id(0)]
    p = softmax_rows(halves(q_ref[0]), k_ref[0], length)
    o_ref[0] = merge(dot(p.astype(BF16), v_ref[0], 1, 0)).astype(BF16)


def attend(first, lengths, q, k, v):
    n, rows, width = q.shape
    keys = k.shape[1]
    return pl.pallas_call(
        attend_kernel,
        grid_spec=pltpu.PrefetchScalarGridSpec(
            num_scalar_prefetch=2,
            grid=(n, width // PAIR),
            in_specs=[
                pl.BlockSpec((1, rows, PAIR), lambda s, h, f, l: (s, 0, h)),
                pl.BlockSpec((1, keys, PAIR), lambda s, h, f, l: (f[0] + s, 0, h)),
                pl.BlockSpec((1, keys, PAIR), lambda s, h, f, l: (f[0] + s, 0, h)),
            ],
            out_specs=pl.BlockSpec((1, rows, PAIR), lambda s, h, f, l: (s, 0, h)),
        ),
        out_shape=jax.ShapeDtypeStruct(q.shape, BF16),
        cost_estimate=pl.CostEstimate(
            flops=4 * n * rows * keys * width * 4, bytes_accessed=4 * n * (rows + keys) * width,
            transcendentals=n * rows * keys * width // HD,
        ),
        name="attend",
    )(first, lengths, q, k, v)


def attend_back_kernel(lengths_ref, q_ref, k_ref, v_ref, g_ref, dq_ref, dk_ref, dv_ref):
    length = lengths_ref[pl.program_id(0)]
    q = halves(q_ref[0])
    g = halves(g_ref[0])
    k = k_ref[0]
    p = softmax_rows(q, k, length)
    dv_ref[0] = dot(p.astype(BF16), g, 0, 0).astype(BF16)
    dp = dot(g, v_ref[0], 1, 1)
    ds = p * (dp - jnp.sum(dp * p, axis=-1, keepdims=True))
    ds = (ds * SCALE).astype(BF16)
    dq_ref[0] = merge(dot(ds, k, 1, 0)).astype(BF16)
    dk_ref[0] = dot(ds, q, 0, 0).astype(BF16)


def attend_back(lengths, q, k, v, g):
    n, rows, width = q.shape
    keys = k.shape[1]
    q_spec = pl.BlockSpec((1, rows, PAIR), lambda s, h, l: (s, 0, h))
    k_spec = pl.BlockSpec((1, keys, PAIR), lambda s, h, l: (s, 0, h))
    return pl.pallas_call(
        attend_back_kernel,
        grid_spec=pltpu.PrefetchScalarGridSpec(
            num_scalar_prefetch=1,
            grid=(n, width // PAIR),
            in_specs=[q_spec, k_spec, k_spec, q_spec],
            out_specs=[q_spec, k_spec, k_spec],
        ),
        out_shape=[
            jax.ShapeDtypeStruct(q.shape, BF16),
            jax.ShapeDtypeStruct(k.shape, BF16),
            jax.ShapeDtypeStruct(k.shape, BF16),
        ],
        cost_estimate=pl.CostEstimate(
            flops=10 * n * rows * keys * width * 4, bytes_accessed=4 * n * (rows + 2 * keys) * width,
            transcendentals=n * rows * keys * width // HD,
        ),
        name="attend_back",
    )(lengths, q, k, v, g)


def norm_parts(y):
    centered = y - jnp.mean(y, axis=-1, keepdims=True)
    rstd = lax.rsqrt(jnp.mean(centered * centered, axis=-1, keepdims=True) + EPS)
    return centered * rstd, rstd


def norm_back(grad, gain, hat, rstd):
    scaled = grad * gain
    return rstd * (
        scaled
        - jnp.mean(scaled, axis=-1, keepdims=True)
        - hat * jnp.mean(scaled * hat, axis=-1, keepdims=True)
    )


def mm(a, b):
    return jnp.dot(a, b, preferred_element_type=F32)


def mm_nt(a, b):
    return lax.dot_general(a, b, (((1,), (1,)), ((), ())), preferred_element_type=F32)


def mm_tn(a, b):
    return lax.dot_general(a, b, (((0,), (0,)), ((), ())), preferred_element_type=F32)


def gather_rows(one, ranks, copies, which, *parts):
    shares = [p.reshape(copies, p.shape[0] // copies, p.shape[1]) for p in parts]
    mine = jnp.concatenate(
        [lax.dynamic_index_in_dim(s, which, 0, keepdims=False) for s in shares], axis=0
    ).astype(F32)
    whole = lax.all_gather(mine, ("tensor", "dp"), tiled=False) * one
    whole = whole.reshape(ranks, copies, mine.shape[0], mine.shape[1])
    out, at = [], 0
    for s in shares:
        out.append(
            whole[:, :, at : at + s.shape[1]].astype(BF16).reshape(ranks, copies * s.shape[1], s.shape[2])
        )
        at += s.shape[1]
    return out


def body(
    ranks, copies, tokens, w_qkv, b_qv, w_out, b_out, ln1_gain, ln1_bias, w_up, b_up, w_down, b_down,
    ln2_gain, ln2_bias, lengths, picks, cotangent,
):
    rank = lax.axis_index("tensor")
    which = lax.axis_index("dp")
    seqs = lengths.shape[0]
    rows, width = tokens.shape
    seq = rows // seqs
    slots = picks.shape[1]
    part = w_qkv.shape[2]
    hidden = w_up.shape[1]
    own = seqs // ranks

    one = jnp.where(lengths[0] > 0, 1.0, 0.0).astype(F32)

    own_qkv = jnp.swapaxes(w_qkv, 1, 2).reshape(3 * part, width)
    (all_qkv,) = gather_rows(one, ranks, copies, which, own_qkv)
    all_qkv = jnp.swapaxes(all_qkv.reshape(ranks, 3, part, width), 0, 1).reshape(3, ranks * part, width)
    all_out, all_up, all_down = gather_rows(one, ranks, copies, which, w_out, w_up, w_down)
    all_out = all_out.reshape(ranks * part, width)
    all_down = all_down.reshape(ranks * hidden, width)
    all_up = jnp.swapaxes(all_up, 0, 1).reshape(width, ranks * hidden)
    vectors = lax.all_gather(jnp.concatenate([b_qv.reshape(-1), b_up]), "tensor")
    all_b_qv = jnp.swapaxes(vectors[:, : 2 * part].reshape(ranks, 2, part), 0, 1).reshape(2, ranks * part)
    all_b_up = vectors[:, 2 * part :].reshape(-1)

    by_seq = tokens.reshape(seqs, seq, width)
    chosen = (picks[:, :, None] == jnp.arange(seq)[None, None, :])
    chosen_low = chosen.astype(BF16)
    chosen_f32 = chosen.astype(F32)
    picked = jnp.einsum("spk,skd->spd", chosen_low, by_seq, preferred_element_type=F32).astype(BF16)
    grad_output = jnp.einsum(
        "spk,skd->spd", chosen_f32, cotangent.reshape(seqs, seq, width),
        precision=lax.Precision.HIGH, preferred_element_type=F32,
    ).reshape(seqs * slots, width)
    first = rank * own
    own_tokens = lax.dynamic_slice_in_dim(tokens, first * seq, own * seq, 0)
    n_own = own * seq
    used = jnp.concatenate([own_tokens, picked.reshape(seqs * slots, width)], axis=0)

    keys = mm_nt(tokens, all_qkv[1]).astype(BF16).reshape(seqs, seq, width)
    values = (mm_nt(tokens, all_qkv[2]) + all_b_qv[1]).astype(BF16).reshape(seqs, seq, width)
    queries = (mm_nt(used, all_qkv[0]) + all_b_qv[0]).astype(BF16)
    q_picked = queries[n_own:].reshape(seqs, slots, width)
    zero = jnp.zeros((1,), jnp.int32)
    att_own = attend(first.reshape(1), lengths, queries[:n_own].reshape(own, seq, width), keys, values)
    att_picked = attend(zero, lengths, q_picked, keys, values)
    attended = jnp.concatenate([att_own.reshape(n_own, width), att_picked.reshape(-1, width)], axis=0)

    first_sum = used.astype(F32) + mm(attended, all_out) + b_out
    hat1, rstd1 = norm_parts(first_sum)
    normed = hat1 * ln1_gain + ln1_bias
    normed_low = normed.astype(BF16)
    inner = mm(normed_low, all_up) + all_b_up
    cdf = 0.5 * (1.0 + lax.erf(inner * 0.7071067811865476))
    active = (inner * cdf).astype(BF16)
    second_sum = normed + mm(active, all_down) + b_down
    hat2, rstd2 = norm_parts(second_sum)
    out_own = hat2[:n_own] * ln2_gain + ln2_bias
    output = (lax.all_gather(out_own, "tensor", tiled=True) * one).astype(BF16)

    hat2, rstd2, hat1, rstd1 = hat2[n_own:], rstd2[n_own:], hat1[n_own:], rstd1[n_own:]
    inner, cdf, active, normed_low = inner[n_own:], cdf[n_own:], active[n_own:], normed_low[n_own:]
    att = attended[n_own:]
    grad_second = norm_back(grad_output, ln2_gain, hat2, rstd2)
    g_ln2_gain = jnp.sum(grad_output * hat2, axis=0)
    g_ln2_bias = jnp.sum(grad_output, axis=0)
    g_b_down = jnp.sum(grad_second, axis=0)
    second_low = grad_second.astype(BF16)
    own_hidden = lambda x: lax.dynamic_slice_in_dim(x, rank * hidden, hidden, 1)
    own_part = lambda x: lax.dynamic_slice_in_dim(x, rank * part, part, x.ndim - 1)
    g_w_down = lax.psum(mm_tn(own_hidden(active), second_low), "dp")
    grad_active = mm_nt(second_low, all_down)
    slope = cdf + inner * (0.3989422804014327 * jnp.exp(-0.5 * inner * inner))
    grad_inner = (grad_active * slope).astype(BF16)
    own_inner = own_hidden(grad_inner)
    g_b_up = jnp.sum(own_inner, axis=0, dtype=F32)
    g_w_up = lax.psum(mm_tn(normed_low, own_inner), "dp")
    grad_normed = grad_second + mm_nt(grad_inner, all_up)
    grad_first = norm_back(grad_normed, ln1_gain, hat1, rstd1)
    g_ln1_gain = jnp.sum(grad_normed * hat1, axis=0)
    g_ln1_bias = jnp.sum(grad_normed, axis=0)
    g_b_out = jnp.sum(grad_first, axis=0)
    first_low = grad_first.astype(BF16)
    g_w_out = lax.psum(mm_tn(own_part(att), first_low), "dp")
    grad_att = mm_nt(first_low, all_out).astype(BF16)
    dq, dk, dv = attend_back(lengths, q_picked, keys, values, grad_att.reshape(seqs, slots, width))
    dq_rows = dq.reshape(seqs * slots, width)
    dk_rows = dk.reshape(rows, width)
    dv_rows = dv.reshape(rows, width)
    sparse = (grad_first + mm(dq_rows, all_qkv[0])).reshape(seqs, slots, width)
    grad_tokens = (
        jnp.einsum("spk,spd->skd", chosen_f32, sparse, precision=lax.Precision.HIGH,
                   preferred_element_type=F32).reshape(rows, width)
        + mm(dk_rows, all_qkv[1])
        + mm(dv_rows, all_qkv[2])
    )
    own_q, own_k, own_v = own_part(dq_rows), own_part(dk_rows), own_part(dv_rows)
    g_w_qkv = jnp.stack([
        mm_tn(picked.reshape(seqs * slots, width), own_q), mm_tn(tokens, own_k), mm_tn(tokens, own_v),
    ])
    g_b_qv = jnp.stack([jnp.sum(own_q, axis=0, dtype=F32), jnp.sum(own_v, axis=0, dtype=F32)])
    g_w_qkv, g_b_qv, g_b_out, g_ln1_gain, g_ln1_bias, g_b_up, g_b_down, g_ln2_gain, g_ln2_bias = lax.psum(
        (g_w_qkv, g_b_qv, g_b_out, g_ln1_gain, g_ln1_bias, g_b_up, g_b_down, g_ln2_gain, g_ln2_bias), "dp"
    )
    return (
        output, grad_tokens, g_w_qkv, g_b_qv, g_w_out, g_b_out, g_ln1_gain, g_ln1_bias, g_w_up, g_b_up,
        g_w_down, g_b_down, g_ln2_gain, g_ln2_bias,
    )


def solution(mesh):
    in_specs = (
        P("dp", None), P(None, None, "tensor"), P(None, "tensor"), P("tensor", None), P(), P(), P(),
        P(None, "tensor"), P("tensor"), P("tensor", None), P(), P(), P(), P("dp"), P("dp", None), P("dp", None),
    )
    out_specs = (
        P("dp", None), P("dp", None), P(None, None, "tensor"), P(None, "tensor"), P("tensor", None), P(), P(),
        P(), P(None, "tensor"), P("tensor"), P("tensor", None), P(), P(), P(),
    )
    step = functools.partial(body, mesh.shape["tensor"], mesh.shape["dp"])
    return jax.shard_map(step, mesh=mesh, in_specs=in_specs, out_specs=out_specs, check_vma=False)
```

```python
import functools

import jax
import jax.numpy as jnp
from jax import lax
from jax.experimental import pallas as pl
from jax.experimental.pallas import tpu as pltpu
from jax.sharding import PartitionSpec as P

HD = 64
PAIR = 2 * HD
EPS = 1e-05
SCALE = 0.125
NEG = -1e30
F32 = jnp.float32
BF16 = jnp.bfloat16
GROUP = 8
MESH_ID = pl.DeviceIdType.MESH
VMEM = 56 * 2**20


def dot(a, b, ca, cb):
    return lax.dot_general(a, b, (((ca,), (cb,)), ((), ())), preferred_element_type=F32)


def halves(block):
    lane = lax.broadcasted_iota(jnp.int32, block.shape, 1)
    zero = jnp.zeros_like(block)
    return jnp.concatenate([jnp.where(lane < HD, block, zero), jnp.where(lane < HD, zero, block)], axis=0)


def merge(stacked):
    rows = stacked.shape[0] // 2
    lane = lax.broadcasted_iota(jnp.int32, (rows, PAIR), 1)
    return jnp.where(lane < HD, stacked[:rows], stacked[rows:])


def scores_of(stacked_q, keys, length):
    scores = dot(stacked_q * SCALE, keys, 1, 1)
    key_at = lax.broadcasted_iota(jnp.int32, (1, keys.shape[0]), 1)
    scores = scores + jnp.where(key_at < length, 0.0, NEG)
    return jnp.exp(scores - jnp.max(scores, axis=-1, keepdims=True))


def softmax_rows(stacked_q, keys, length):
    e = scores_of(stacked_q, keys, length)
    return e / jnp.sum(e, axis=-1, keepdims=True)


def attend_pair(q, k, v, length):
    e = scores_of(halves(q), k, length)
    total = jnp.sum(e, axis=-1, keepdims=True)
    return merge(dot(e.astype(BF16), v, 1, 0) / total).astype(BF16)


def flip(w, bit):
    return w + bit - 2 * bit * lax.rem(w // bit, 2)


def turn(z, k):
    b0, b1 = lax.rem(z, 2), lax.rem(z // 2, 2)
    return z + (k & 1) * (1 - 2 * b0) + (k >> 1) * (2 - 4 * b1)


def front_kernel(
    ranks, chunks, x_ref, xp_ref, mine_ref, lengths_ref, head_ref, tail_ref, vec_ref,
    k_ref, v_ref, qp_ref, a_ref, out_ref, vecs_ref, w_ref,
    heads_ref, q_ref, zs, zr, xs, xr, ys, yr, ds, dr, es, er, cs, cr, ss, sr,
):
    w, z = lax.axis_index("dp"), lax.axis_index("tensor")
    low = lax.rem(w, GROUP)
    wc, wx, wy = flip(w, 1), flip(w, 2), flip(w, 4)
    share = lambda dev: lax.rem(dev, GROUP)
    across = share(flip(wx, 4))
    zk = {k: turn(z, k) for k in range(1, ranks)}
    barrier = pltpu.get_barrier_semaphore()
    peers = [{"dp": w, "tensor": zk[k]} for k in zk] + [{"dp": d, "tensor": z} for d in (wc, wx, wy)]
    for peer in peers:
        pl.semaphore_signal(barrier, inc=1, device_id=peer, device_id_type=MESH_ID)
    pl.semaphore_wait(barrier, len(peers))

    def remote(src, dst, s, r, to_w, to_z):
        return pltpu.make_async_remote_copy(
            src_ref=src, dst_ref=dst, send_sem=s, recv_sem=r,
            device_id={"dp": to_w, "tensor": to_z}, device_id_type=MESH_ID,
        )

    items = [(k, True, 0, head_ref.shape[0]) for k in zk] + [(k, False, at, n) for at, n in chunks for k in zk]

    def land(i, rank, sh, at, n):
        return (heads_ref if items[i][1] else out_ref).at[rank, sh, pl.ds(at, n)]

    def copy(i, what):
        k, _, at, n = items[i]
        h = (n // 2 + 7) // 8 * 8
        if what == "z":
            src = head_ref if items[i][1] else tail_ref
            return remote(src.at[pl.ds(at, n)], land(i, z, low, at, n), zs.at[i], zr.at[i], w, zk[k])
        sh, at, n, s, r, to = {
            "x": (low, at, n, xs.at[i], xr.at[i], wx),
            "y": (low, at, n, ys.at[i], yr.at[i], wy),
            "d": (share(wx), at, h, ds.at[i], dr.at[i], wy),
            "e": (share(wy), at + h, n - h, es.at[i], er.at[i], wx),
            0: (low, at, n, cs.at[i, 0], cr.at[i, 0], wc),
            1: (share(wx), at, n, cs.at[i, 1], cr.at[i, 1], wc),
            2: (share(wy), at, n, cs.at[i, 2], cr.at[i, 2], wc),
            3: (across, at, n, cs.at[i, 3], cr.at[i, 3], wc),
        }[what]
        ref = land(i, zk[k], sh, at, n)
        return remote(ref, ref, s, r, to, z)

    def vector_copy(k):
        return remote(vec_ref, vecs_ref.at[z], ss.at[k - 1], sr.at[k - 1], w, zk[k])

    follows = (("z", ("x", "y", 0)), ("x", ("d", 1)), ("y", ("e", 2)), ("d", ()), ("e", (3,)))
    stages = (follows[:1], follows[1:3], follows[3:])

    def steps(first, last, t):
        for lag, stage in enumerate(stages):
            i = t + first - lag
            if first <= i < last:
                for arrived, onward in stage:
                    copy(i, arrived).wait_recv()
                    for what in onward:
                        copy(i, what).start()

    for i in range(len(items)):
        copy(i, "z").start()
        if i == ranks - 2:
            for k in zk:
                vector_copy(k).start()
    nh = ranks - 1
    for t in range(nh + 2):
        steps(0, nh, t)
    for i in range(nh):
        for j in range(4):
            copy(i, j).wait_recv()
    for k in zk:
        vector_copy(k).wait_recv()
    vecs_ref[z] = vec_ref[...]

    part = mine_ref.shape[0] // 3
    for r in range(ranks):
        block = heads_ref[r].reshape(3 * part, -1)
        for i in range(3):
            w_ref[i, r * part : (r + 1) * part] = block[i * part : (i + 1) * part].astype(BF16)
    at = pl.multiple_of(z * part, part)
    for i in range(3):
        w_ref[i, pl.ds(at, part)] = mine_ref[i * part : (i + 1) * part]
    vectors = vecs_ref[0]
    for r in range(1, ranks):
        vectors = vectors + vecs_ref[r]
    bias_q, bias_v = vectors[1:2], vectors[2:3]

    seqs, _, width = x_ref.shape
    pairs = width // PAIR
    rounds = len(items) - nh + 2
    space = seqs * pairs // rounds

    def compute(t, carry):
        for j in range(rounds):
            @pl.when(t == j * space)
            def _():
                steps(nh, len(items), j)

        s, h = t // pairs, lax.rem(t, pairs)

        @pl.when(h == 0)
        def _():
            x = x_ref[s]
            k_ref[s] = dot(x, w_ref[1], 1, 1).astype(BF16)
            v_ref[s] = (dot(x, w_ref[2], 1, 1) + bias_v).astype(BF16)
            q_ref[...] = (dot(x, w_ref[0], 1, 1) + bias_q).astype(BF16)
            qp_ref[s] = (dot(xp_ref[s], w_ref[0], 1, 1) + bias_q).astype(BF16)

        cols = pl.ds(pl.multiple_of(h * PAIR, PAIR), PAIR)
        a_ref[s, :, cols] = attend_pair(q_ref[:, cols], k_ref[s, :, cols], v_ref[s, :, cols], lengths_ref[s])
        return carry

    lax.fori_loop(0, seqs * pairs, compute, 0)
    for i in range(nh, len(items)):
        for j in range(4):
            copy(i, j).wait_recv()
    for i in range(len(items)):
        for what in ("z", "x", "y", "d", "e", 0, 1, 2, 3):
            copy(i, what).wait_send()
    for k in zk:
        vector_copy(k).wait_send()


def front(ranks, chunks, x, xp, mine, lengths, head, tail, vectors):
    seqs, seq, width = x.shape
    n = (ranks - 1) * (len(chunks) + 1)
    dma = pltpu.SemaphoreType.DMA
    vmem = pl.BlockSpec(memory_space=pltpu.VMEM)
    any_space = pl.BlockSpec(memory_space=pl.ANY)
    shape = jax.ShapeDtypeStruct
    return pl.pallas_call(
        functools.partial(front_kernel, ranks, chunks),
        out_shape=[
            shape(x.shape, BF16), shape(x.shape, BF16), shape(xp.shape, BF16), shape(x.shape, BF16),
            shape((ranks, GROUP) + tail.shape, F32), shape((ranks,) + vectors.shape, F32),
            shape((3, width, width), BF16),
        ],
        in_specs=[vmem] * 3 + [pl.BlockSpec(memory_space=pltpu.SMEM)] + [any_space] * 2 + [vmem],
        out_specs=[vmem] * 4 + [any_space, vmem, vmem],
        scratch_shapes=[
            pltpu.VMEM((ranks, GROUP) + head.shape, F32), pltpu.VMEM((seq, width), BF16),
        ] + [dma((n,))] * 10 + [dma((n, 4))] * 2 + [dma((ranks - 1,))] * 2,
        compiler_params=pltpu.CompilerParams(collective_id=1, has_side_effects=True, vmem_limit_bytes=VMEM),
        name="front",
    )(x, xp, mine, lengths, head, tail, vectors)


def attend_back_kernel(lengths_ref, q_ref, k_ref, v_ref, g_ref, dq_ref, dk_ref, dv_ref):
    length = lengths_ref[pl.program_id(0)]
    q = halves(q_ref[0])
    g = halves(g_ref[0])
    k = k_ref[0]
    p = softmax_rows(q, k, length)
    dv_ref[0] = dot(p.astype(BF16), g, 0, 0).astype(BF16)
    dp = dot(g, v_ref[0], 1, 1)
    ds = p * (dp - jnp.sum(dp * p, axis=-1, keepdims=True))
    ds = (ds * SCALE).astype(BF16)
    dq_ref[0] = merge(dot(ds, k, 1, 0)).astype(BF16)
    dk_ref[0] = dot(ds, q, 0, 0).astype(BF16)


def attend_back(lengths, q, k, v, g):
    n, rows, width = q.shape
    keys = k.shape[1]
    q_spec = pl.BlockSpec((1, rows, PAIR), lambda s, h, l: (s, 0, h))
    k_spec = pl.BlockSpec((1, keys, PAIR), lambda s, h, l: (s, 0, h))
    return pl.pallas_call(
        attend_back_kernel,
        grid_spec=pltpu.PrefetchScalarGridSpec(
            num_scalar_prefetch=1,
            grid=(n, width // PAIR),
            in_specs=[q_spec, k_spec, k_spec, q_spec],
            out_specs=[q_spec, k_spec, k_spec],
        ),
        out_shape=[
            jax.ShapeDtypeStruct(q.shape, BF16),
            jax.ShapeDtypeStruct(k.shape, BF16),
            jax.ShapeDtypeStruct(k.shape, BF16),
        ],
        cost_estimate=pl.CostEstimate(
            flops=10 * n * rows * keys * width * 4, bytes_accessed=4 * n * (rows + 2 * keys) * width,
            transcendentals=n * rows * keys * width // HD,
        ),
        name="attend_back",
    )(lengths, q, k, v, g)


def norm_parts(y):
    centered = y - jnp.mean(y, axis=-1, keepdims=True)
    rstd = lax.rsqrt(jnp.mean(centered * centered, axis=-1, keepdims=True) + EPS)
    return centered * rstd, rstd


def norm_back(grad, gain, hat, rstd):
    scaled = grad * gain
    return rstd * (
        scaled
        - jnp.mean(scaled, axis=-1, keepdims=True)
        - hat * jnp.mean(scaled * hat, axis=-1, keepdims=True)
    )


def mm(a, b):
    return jnp.dot(a, b, preferred_element_type=F32)


def mm_nt(a, b):
    return lax.dot_general(a, b, (((1,), (1,)), ((), ())), preferred_element_type=F32)


def mm_tn(a, b):
    return lax.dot_general(a, b, (((0,), (0,)), ((), ())), preferred_element_type=F32)


def reduce_kernel(chunks, n_in, *refs):
    ins, outs = refs[:n_in], refs[n_in:2 * n_in]
    acc_ref, halves_ref, quarter_ref, eighth_ref, send_sem, recv_sem = refs[2 * n_in:]
    w = lax.axis_index("dp")
    z = lax.axis_index("tensor")
    bit = {"c": lax.rem(w, 2), "x": lax.rem(w // 2, 2), "y": lax.rem(w // 4, 2)}
    peer = {"c": flip(w, 1), "x": flip(w, 2), "y": flip(w, 4)}
    barrier = pltpu.get_barrier_semaphore()
    for p in peer.values():
        pl.semaphore_signal(barrier, inc=1, device_id={"dp": p, "tensor": z}, device_id_type=MESH_ID)
    pl.semaphore_wait(barrier, 3)
    def send(c, j, axis, src, dst):
        copy = pltpu.make_async_remote_copy(src_ref=src, dst_ref=dst, send_sem=send_sem.at[c, j], recv_sem=recv_sem.at[c, j],
            device_id={"dp": peer[axis], "tensor": z}, device_id_type=MESH_ID)
        copy.start()
        return copy
    def at(ref, start, n):
        return ref.at[pl.ds(pl.multiple_of(start, 8), n)]
    def add(dst, d_at, a, a_at, b, b_at, n):
        step = 16 if n % 16 == 0 else 8
        def body(i, carry):
            o = i * step
            dst[pl.ds(pl.multiple_of(d_at + o, 8), step)] = (
                a[pl.ds(pl.multiple_of(a_at + o, 8), step)] + b[pl.ds(pl.multiple_of(b_at + o, 8), step)])
            return carry
        lax.fori_loop(0, n // step, body, 0)
    copies = {}
    h_at = 0
    base = []
    for (r, o, n) in chunks:
        base.append(h_at); h_at += n
    def stage(c, s):
        r, o, n = chunks[c]
        x, out = ins[r], outs[r]
        hb, qb, eb = base[c] // 2, base[c] // 4, base[c] // 8
        half = o + bit["c"] * (n // 2)
        other = o + (1 - bit["c"]) * (n // 2)
        q, e, f = n // 4, n // 8, n // 16
        streams = (("x", "y"), ("y", "x"))
        if s == 0:
            copies[c, 0] = send(c, 0, "c", at(x, other, n // 2), halves_ref.at[pl.ds(hb, n // 2)])
        elif s == 1:
            copies[c, 0].wait_recv()
            add(acc_ref, hb, x, half, halves_ref, hb, n // 2)
            for i, (p, _) in enumerate(streams):
                copies[c, 1 + i] = send(c, 1 + i, p, at(acc_ref, hb + i * q + (1 - bit[p]) * e, e), quarter_ref.at[pl.ds(qb + i * e, e)])
        elif s == 2:
            for i, (p, p2) in enumerate(streams):
                copies[c, 1 + i].wait_recv()
                a0 = hb + i * q + bit[p] * e
                add(acc_ref, a0, acc_ref, a0, quarter_ref, qb + i * e, e)
                copies[c, 3 + i] = send(c, 3 + i, p2, at(acc_ref, a0 + (1 - bit[p2]) * f, f), eighth_ref.at[pl.ds(eb + i * f, f)])
        elif s == 3:
            for i, (p, p2) in enumerate(streams):
                copies[c, 3 + i].wait_recv()
                a1 = i * q + bit[p] * e + bit[p2] * f
                add(out, half + a1, acc_ref, hb + a1, eighth_ref, eb + i * f, f)
                a1 = half + a1
                copies[c, 5 + i] = send(c, 5 + i, p2, at(out, a1, f), at(out, a1, f))
        elif s == 4:
            for i, (p, p2) in enumerate(streams):
                copies[c, 5 + i].wait_recv()
                a0 = half + i * q + bit[p] * e
                copies[c, 7 + i] = send(c, 7 + i, p, at(out, a0, e), at(out, a0, e))
        elif s == 5:
            for i in range(2):
                copies[c, 7 + i].wait_recv()
            copies[c, 9] = send(c, 9, "c", at(out, half, n // 2), at(out, half, n // 2))
        else:
            copies[c, 9].wait_recv()
    for t in range(len(chunks) + 6):
        for s in range(7):
            if 0 <= t - s < len(chunks):
                stage(t - s, s)
    for copy in copies.values():
        copy.wait_send()

def dp_reduce(outer, arrays, step, cid):
    chunks = []
    for r, a in enumerate(arrays):
        for o in range(0, a.shape[0], step):
            chunks.append((r, o, min(step, a.shape[0] - o)))
    total = sum(n for _, _, n in chunks)
    width = arrays[0].shape[1]
    vmem = lambda rows: pltpu.VMEM((rows, width), F32)
    dma = pltpu.SemaphoreType.DMA((len(chunks), 10))
    spec = pl.BlockSpec(memory_space=pltpu.VMEM)
    sums = pl.pallas_call(
        functools.partial(reduce_kernel, tuple(chunks), len(arrays)),
        out_shape=[jax.ShapeDtypeStruct(a.shape, F32) for a in arrays],
        in_specs=[spec] * len(arrays), out_specs=[spec] * len(arrays),
        scratch_shapes=[vmem(total // 2), vmem(total // 2), vmem(total // 4), vmem(total // 8), dma, dma],
        compiler_params=pltpu.CompilerParams(collective_id=cid, has_side_effects=True, vmem_limit_bytes=VMEM),
        name="dp_reduce",
    )(*arrays)
    if outer is not None:
        sums = [lax.psum(a, "dp", axis_index_groups=outer) for a in sums]
    return sums


def my_share(which, p):
    return lax.dynamic_index_in_dim(
        p.reshape(GROUP, p.shape[0] // GROUP, p.shape[1]), lax.rem(which, GROUP), 0, keepdims=False
    )


def body(
    ranks, outer, tokens, w_qkv, b_qv, w_out, b_out, ln1_gain, ln1_bias, w_up, b_up, w_down, b_down,
    ln2_gain, ln2_bias, lengths, picks, cotangent,
):
    rank = lax.axis_index("tensor")
    which = lax.axis_index("dp")
    seqs = lengths.shape[0]
    rows, width = tokens.shape
    seq = rows // seqs
    slots = picks.shape[1]
    part = w_qkv.shape[2]
    hidden = w_up.shape[1]

    by_seq = tokens.reshape(seqs, seq, width)
    chosen = (picks[:, :, None] == jnp.arange(seq)[None, None, :])
    chosen_low = chosen.astype(BF16)
    chosen_f32 = chosen.astype(F32)
    picked = jnp.einsum("spk,skd->spd", chosen_low, by_seq, preferred_element_type=F32).astype(BF16)
    picked_rows = picked.reshape(seqs * slots, width)

    own_qkv = jnp.swapaxes(w_qkv, 1, 2).reshape(3 * part, width)
    row_out, row_up, row_down = w_out.shape[0] // GROUP, hidden // GROUP, hidden // GROUP
    head = my_share(which, own_qkv).astype(F32)
    tail = jnp.concatenate([my_share(which, p) for p in (w_out, w_up.T, w_down)], axis=0).astype(F32)
    spots = lax.dynamic_update_slice_in_dim(jnp.zeros((2, width), F32), b_qv, rank * part, 1)
    vectors = jnp.concatenate([b_up.reshape(1, width), spots, jnp.zeros((5, width), F32)], axis=0)
    cut = row_out + row_up
    keys, values, q_picked, attended, gathered, all_vectors, all_qkv = front(
        ranks, ((0, cut), (cut, row_down)), by_seq, picked, own_qkv, lengths, head, tail, vectors
    )
    all_b_up = all_vectors[:, 0].reshape(-1)

    def whole(at, n, mine):
        block = gathered[:, :, at : at + n].astype(BF16).reshape(ranks, GROUP * n, width)
        return lax.dynamic_update_index_in_dim(block, mine, rank, 0).reshape(-1, width)

    all_out = whole(0, row_out, w_out)
    all_up = whole(row_out, row_up, w_up.T)
    all_down = whole(cut, row_down, w_down)
    att_picked = jnp.einsum("spk,skd->spd", chosen_low, attended, preferred_element_type=F32).astype(BF16)
    grad_output = jnp.einsum(
        "spk,skd->spd", chosen_f32, cotangent.reshape(seqs, seq, width),
        precision=lax.Precision.HIGH, preferred_element_type=F32,
    ).reshape(seqs * slots, width)
    def forward(tok, att):
        first_sum = tok.astype(F32) + mm(att, all_out) + b_out
        hat1, rstd1 = norm_parts(first_sum)
        normed = hat1 * ln1_gain + ln1_bias
        normed_low = normed.astype(BF16)
        inner = mm_nt(normed_low, all_up) + all_b_up
        cdf = 0.5 * (1.0 + lax.erf(inner * 0.7071067811865476))
        active = (inner * cdf).astype(BF16)
        hat2, rstd2 = norm_parts(normed + mm(active, all_down) + b_down)
        return hat1, rstd1, normed_low, inner, cdf, active, hat2, rstd2

    output = (forward(tokens, attended.reshape(rows, width))[6] * ln2_gain + ln2_bias).astype(BF16)

    att = att_picked.reshape(-1, width)
    hat1, rstd1, normed_low, inner, cdf, active, hat2, rstd2 = forward(picked_rows, att)
    grad_second = norm_back(grad_output, ln2_gain, hat2, rstd2)
    g_ln2_gain = jnp.sum(grad_output * hat2, axis=0)
    g_ln2_bias = jnp.sum(grad_output, axis=0)
    g_b_down = jnp.sum(grad_second, axis=0)
    second_low = grad_second.astype(BF16)
    own_hidden = lambda x: lax.dynamic_slice_in_dim(x, rank * hidden, hidden, 1)
    own_part = lambda x: lax.dynamic_slice_in_dim(x, rank * part, part, x.ndim - 1)
    g_w_down = mm_tn(own_hidden(active), second_low)
    grad_active = mm_nt(second_low, all_down)
    slope = cdf + inner * (0.3989422804014327 * jnp.exp(-0.5 * inner * inner))
    grad_inner = (grad_active * slope).astype(BF16)
    own_inner = own_hidden(grad_inner)
    g_b_up = jnp.sum(own_inner, axis=0, dtype=F32)
    g_w_up = mm_tn(normed_low, own_inner)
    grad_normed = grad_second + mm(grad_inner, all_up)
    grad_first = norm_back(grad_normed, ln1_gain, hat1, rstd1)
    g_ln1_gain = jnp.sum(grad_normed * hat1, axis=0)
    g_ln1_bias = jnp.sum(grad_normed, axis=0)
    g_b_out = jnp.sum(grad_first, axis=0)
    first_low = grad_first.astype(BF16)
    g_w_out = mm_tn(own_part(att), first_low)
    grad_att = mm_nt(first_low, all_out).astype(BF16)
    dq, dk, dv = attend_back(lengths, q_picked, keys, values, grad_att.reshape(seqs, slots, width))
    dq_rows = dq.reshape(seqs * slots, width)
    dk_rows = dk.reshape(rows, width)
    dv_rows = dv.reshape(rows, width)
    own_q, own_k, own_v = own_part(dq_rows), own_part(dk_rows), own_part(dv_rows)
    g_b_qv = jnp.concatenate([jnp.sum(own_q, axis=0, dtype=F32), jnp.sum(own_v, axis=0, dtype=F32)])
    g_vectors = jnp.concatenate([
        g_b_out, g_ln1_gain, g_ln1_bias, g_b_down, g_ln2_gain, g_ln2_bias, g_b_up, g_b_qv,
        jnp.zeros((8 * width - 6 * width - hidden - 2 * part,), F32),
    ]).reshape(8, width)
    used_rows = part + 3 * part + 8
    g_last = jnp.concatenate([
        g_w_out, mm_tn(own_q, picked_rows), mm_tn(own_k, tokens), mm_tn(own_v, tokens), g_vectors,
        jnp.zeros((-used_rows % 128, width), F32),
    ], axis=0)
    g_w_down, g_w_up, g_last = dp_reduce(outer, [g_w_down, g_w_up, g_last], 384, 2)
    g_w_out, g_last = g_last[:part], g_last[part:]
    sparse = (grad_first + mm(dq_rows, all_qkv[0])).reshape(seqs, slots, width)
    grad_tokens = (
        jnp.einsum("spk,spd->skd", chosen_f32, sparse, precision=lax.Precision.HIGH,
                   preferred_element_type=F32).reshape(rows, width)
        + mm(dk_rows, all_qkv[1])
        + mm(dv_rows, all_qkv[2])
    )
    g_w_qkv = jnp.swapaxes(g_last[: 3 * part].reshape(3, part, width), 1, 2)
    g_vectors = g_last[3 * part :].reshape(-1)
    g_b_out, g_ln1_gain, g_ln1_bias, g_b_down, g_ln2_gain, g_ln2_bias = (
        g_vectors[i * width : (i + 1) * width] for i in range(6)
    )
    g_b_up = g_vectors[6 * width : 6 * width + hidden]
    g_b_qv = g_vectors[6 * width + hidden : 6 * width + hidden + 2 * part].reshape(2, part)
    return (
        output, grad_tokens, g_w_qkv, g_b_qv, g_w_out, g_b_out, g_ln1_gain, g_ln1_bias, g_w_up, g_b_up,
        g_w_down, g_b_down, g_ln2_gain, g_ln2_bias,
    )


def solution(mesh):
    in_specs = (
        P("dp", None), P(None, None, "tensor"), P(None, "tensor"), P("tensor", None), P(), P(), P(),
        P(None, "tensor"), P("tensor"), P("tensor", None), P(), P(), P(), P("dp"), P("dp", None), P("dp", None),
    )
    out_specs = (
        P("dp", None), P("dp", None), P(None, None, "tensor"), P(None, "tensor"), P("tensor", None), P(), P(),
        P(), P(None, "tensor"), P("tensor"), P("tensor", None), P(), P(), P(),
    )
    ranks, copies = mesh.shape["tensor"], mesh.shape["dp"]
    outer = None
    if copies > GROUP:
        outer = [[g + j for g in range(0, copies, GROUP)] for j in range(GROUP)]
    step = functools.partial(body, ranks, outer)
    return jax.shard_map(step, mesh=mesh, in_specs=in_specs, out_specs=out_specs, check_vma=False)
```

```python
import functools

import jax
import jax.numpy as jnp
from jax import lax
from jax.experimental import pallas as pl
from jax.experimental.pallas import tpu as pltpu
from jax.sharding import PartitionSpec as P

HD = 64
PAIR = 2 * HD
EPS = 1e-05
SCALE = 0.125
NEG = -1e30
F32 = jnp.float32
BF16 = jnp.bfloat16
GROUP = 8
MESH_ID = pl.DeviceIdType.MESH
VMEM = 56 * 2**20
VMEM_LAST = 62 * 2**20
PACE = 8
SPACE = 9


def dot(a, b, ca, cb):
    return lax.dot_general(a, b, (((ca,), (cb,)), ((), ())), preferred_element_type=F32)


def halves(block):
    lane = lax.broadcasted_iota(jnp.int32, block.shape, 1)
    zero = jnp.zeros_like(block)
    return jnp.concatenate([jnp.where(lane < HD, block, zero), jnp.where(lane < HD, zero, block)], axis=0)


def merge(stacked):
    rows = stacked.shape[0] // 2
    lane = lax.broadcasted_iota(jnp.int32, (rows, PAIR), 1)
    return jnp.where(lane < HD, stacked[:rows], stacked[rows:])


def attend_pair(q, k, v, length):
    key_at = lax.broadcasted_iota(jnp.int32, (1, k.shape[0]), 1)
    mask = jnp.where(key_at < length, 0.0, NEG)
    q_first = lax.broadcasted_iota(jnp.int32, q.shape, 1) < HD
    v_first = lax.broadcasted_iota(jnp.int32, v.shape, 1) < HD
    q = q * SCALE

    def head(q, v):
        scores = dot(q, k, 1, 1) + mask
        e = jnp.exp(scores - jnp.max(scores, axis=-1, keepdims=True))
        return dot(e.astype(BF16), v, 1, 0)

    a = head(jnp.where(q_first, q, jnp.zeros_like(q)), jnp.where(v_first, v, jnp.ones_like(v)))
    b = head(jnp.where(q_first, jnp.zeros_like(q), q), jnp.where(v_first, jnp.ones_like(v), v))
    return (jnp.where(q_first, a, b) / pltpu.roll(jnp.where(q_first, b, a), HD, 1)).astype(BF16)


def flip(w, bit):
    return w + bit - 2 * bit * lax.rem(w // bit, 2)


def turn(z, k):
    b0, b1 = lax.rem(z, 2), lax.rem(z // 2, 2)
    return z + (k & 1) * (1 - 2 * b0) + (k >> 1) * (2 - 4 * b1)


def front_kernel(
    ranks, chunks, space, *refs
):
    x_ref, xp_ref, mine_ref, lengths_ref, head_ref, tail_ref, vec_ref = refs[:7]
    n_w = len(chunks)
    own_refs, refs = refs[7 : 7 + n_w], refs[7 + n_w :]
    k_ref, v_ref, qp_ref, a_ref, out_ref, vecs_ref, w_ref = refs[:7]
    whole_refs, refs = refs[7 : 7 + n_w], refs[7 + n_w :]
    heads_ref, q_ref, wide_ref, low_ref, own_sem, load_sem, store_sem, *sems = refs
    zs, zr, xs, xr, ys, yr, ds, dr, es, er, cs, cr, ss, sr = sems
    w, z = lax.axis_index("dp"), lax.axis_index("tensor")
    low = lax.rem(w, GROUP)
    wc, wx, wy = flip(w, 1), flip(w, 2), flip(w, 4)
    share = lambda dev: lax.rem(dev, GROUP)
    across = share(flip(wx, 4))
    zk = {k: turn(z, k) for k in range(1, ranks)}
    barrier = pltpu.get_barrier_semaphore()
    peers = [{"dp": w, "tensor": zk[k]} for k in zk] + [{"dp": d, "tensor": z} for d in (wc, wx, wy)]
    for peer in peers:
        pl.semaphore_signal(barrier, inc=1, device_id=peer, device_id_type=MESH_ID)
    pl.semaphore_wait(barrier, len(peers))

    def remote(src, dst, s, r, to_w, to_z):
        return pltpu.make_async_remote_copy(
            src_ref=src, dst_ref=dst, send_sem=s, recv_sem=r,
            device_id={"dp": to_w, "tensor": to_z}, device_id_type=MESH_ID,
        )

    items = [(k, None, 0, head_ref.shape[0]) for k in zk]
    items += [(k, c, at, n) for c, (at, n) in enumerate(chunks) for k in zk]

    def land(i, rank, sh, at, n):
        return (heads_ref if items[i][1] is None else out_ref).at[rank, sh, pl.ds(at, n)]

    def copy(i, what):
        k, _, at, n = items[i]
        h = (n // 2 + 7) // 8 * 8
        if what == "z":
            src = head_ref if items[i][1] is None else tail_ref
            return remote(src.at[pl.ds(at, n)], land(i, z, low, at, n), zs.at[i], zr.at[i], w, zk[k])
        sh, at, n, s, r, to = {
            "x": (low, at, n, xs.at[i], xr.at[i], wx),
            "y": (low, at, n, ys.at[i], yr.at[i], wy),
            "d": (share(wx), at, h, ds.at[i], dr.at[i], wy),
            "e": (share(wy), at + h, n - h, es.at[i], er.at[i], wx),
            0: (low, at, n, cs.at[i, 0], cr.at[i, 0], wc),
            1: (share(wx), at, n, cs.at[i, 1], cr.at[i, 1], wc),
            2: (share(wy), at, n, cs.at[i, 2], cr.at[i, 2], wc),
            3: (across, at, n, cs.at[i, 3], cr.at[i, 3], wc),
        }[what]
        ref = land(i, zk[k], sh, at, n)
        return remote(ref, ref, s, r, to, z)

    def vector_copy(k):
        return remote(vec_ref, vecs_ref.at[z], ss.at[k - 1], sr.at[k - 1], w, zk[k])

    follows = (("z", ("x", "y", 0)), ("x", ("d", 1)), ("y", ("e", 2)), ("d", ()), ("e", (3,)))
    stages = (follows[:1], follows[1:3], follows[3:])

    nh = ranks - 1

    def load(i):
        k, _, at, n = items[i]
        slot = i % 2
        return pltpu.make_async_copy(
            out_ref.at[zk[k], :, pl.ds(at, n)], wide_ref.at[slot, :, pl.ds(0, n)], load_sem.at[i - nh]
        )

    def store(i):
        k, c, _, n = items[i]
        to = pl.multiple_of(zk[k] * (GROUP * n), GROUP * n)
        return pltpu.make_async_copy(
            low_ref.at[i % 2, pl.ds(0, GROUP * n)], whole_refs[c].at[pl.ds(to, GROUP * n)], store_sem.at[i - nh]
        )

    def own_store(c):
        n = own_refs[c].shape[0]
        return pltpu.make_async_copy(
            own_refs[c], whole_refs[c].at[pl.ds(pl.multiple_of(z * n, n), n)], own_sem.at[c]
        )

    def steps(t):
        for lag, stage in enumerate(stages):
            i = t - lag
            if 0 <= i < len(items):
                for arrived, onward in stage:
                    copy(i, arrived).wait_recv()
                    for what in onward:
                        copy(i, what).start()
        i = t - 4
        if nh <= i < len(items):
            n = items[i][3]
            load(i).wait()
            if i - 2 >= nh:
                store(i - 2).wait()
            for g in range(GROUP):
                low_ref[i % 2, g * n : (g + 1) * n] = wide_ref[i % 2, g, 0:n].astype(BF16)
            store(i).start()
        i = t - 3
        if nh <= i < len(items):
            for j in range(4):
                copy(i, j).wait_recv()
            load(i).start()

    for c in range(n_w):
        own_store(c).start()
    for i in range(len(items)):
        copy(i, "z").start()
        if i == ranks - 2:
            for k in zk:
                vector_copy(k).start()
    for t in range(nh + 2):
        steps(t)
    for i in range(nh):
        for j in range(4):
            copy(i, j).wait_recv()
    for k in zk:
        vector_copy(k).wait_recv()
    vecs_ref[z] = vec_ref[...]

    part = mine_ref.shape[0] // 3
    for r in range(ranks):
        block = heads_ref[r].reshape(3 * part, -1)
        for i in range(3):
            w_ref[i, r * part : (r + 1) * part] = block[i * part : (i + 1) * part].astype(BF16)
    at = pl.multiple_of(z * part, part)
    for i in range(3):
        w_ref[i, pl.ds(at, part)] = mine_ref[i * part : (i + 1) * part]
    vectors = vecs_ref[0]
    for r in range(1, ranks):
        vectors = vectors + vecs_ref[r]
    bias_q, bias_v = vectors[1:2], vectors[2:3]

    seqs, _, width = x_ref.shape
    pairs = width // PAIR
    rounds = len(items) - nh + 2
    due = [j * space // 4 for j in range(rounds)]

    def compute(t, carry):
        for j in range(rounds):
            @pl.when(t == due[j])
            def _():
                steps(nh + 2 + j)

        s, h = t // pairs, lax.rem(t, pairs)

        @pl.when(h == 0)
        def _():
            x = x_ref[s]
            k_ref[s] = dot(x, w_ref[1], 1, 1).astype(BF16)
            v_ref[s] = (dot(x, w_ref[2], 1, 1) + bias_v).astype(BF16)
            q_ref[...] = (dot(x, w_ref[0], 1, 1) + bias_q).astype(BF16)
            qp_ref[s] = (dot(xp_ref[s], w_ref[0], 1, 1) + bias_q).astype(BF16)

        cols = pl.ds(pl.multiple_of(h * PAIR, PAIR), PAIR)
        a_ref[s, :, cols] = attend_pair(q_ref[:, cols], k_ref[s, :, cols], v_ref[s, :, cols], lengths_ref[s])
        return carry

    lax.fori_loop(0, seqs * pairs, compute, 0)
    for c in range(n_w):
        own_store(c).wait()
    for i in range(len(items) - 2, len(items)):
        store(i).wait()
    for i in range(len(items)):
        for what in ("z", "x", "y", "d", "e", 0, 1, 2, 3):
            copy(i, what).wait_send()
    for k in zk:
        vector_copy(k).wait_send()


def front(ranks, space, x, xp, mine, lengths, head, parts, shares, vectors):
    seqs, seq, width = x.shape
    sizes = [p.shape[0] for p in shares]
    chunks = tuple((sum(sizes[:c]), n) for c, n in enumerate(sizes))
    tail = jnp.concatenate(shares, axis=0)
    rest = (ranks - 1) * len(chunks)
    n = rest + ranks - 1
    dma = pltpu.SemaphoreType.DMA
    vmem = pl.BlockSpec(memory_space=pltpu.VMEM)
    any_space = pl.BlockSpec(memory_space=pl.ANY)
    shape = jax.ShapeDtypeStruct
    return pl.pallas_call(
        functools.partial(front_kernel, ranks, chunks, space),
        out_shape=[
            shape(x.shape, BF16), shape(x.shape, BF16), shape(xp.shape, BF16), shape(x.shape, BF16),
            shape((ranks, GROUP) + tail.shape, F32), shape((ranks,) + vectors.shape, F32),
            shape((3, width, width), BF16),
        ] + [shape((ranks * p.shape[0], width), BF16) for p in parts],
        in_specs=[vmem] * 3 + [pl.BlockSpec(memory_space=pltpu.SMEM)] + [any_space] * 2 + [vmem] * (1 + len(parts)),
        out_specs=[vmem] * 4 + [any_space, vmem, vmem] + [any_space] * len(parts),
        scratch_shapes=[
            pltpu.VMEM((ranks, GROUP) + head.shape, F32), pltpu.VMEM((seq, width), BF16),
            pltpu.VMEM((2, GROUP, max(sizes), width), F32), pltpu.VMEM((2, GROUP * max(sizes), width), BF16),
            dma((len(parts),)), dma((rest,)), dma((rest,)),
        ] + [dma((n,))] * 10 + [dma((n, 4))] * 2 + [dma((ranks - 1,))] * 2,
        compiler_params=pltpu.CompilerParams(collective_id=1, has_side_effects=True, vmem_limit_bytes=VMEM),
        name="front",
    )(x, xp, mine, lengths, head, tail, vectors, *parts)


def attend_back_kernel(lengths_ref, q_ref, k_ref, v_ref, g_ref, dq_ref, dk_ref, dv_ref):
    length = lengths_ref[pl.program_id(0)]
    q = halves(q_ref[0])
    g = halves(g_ref[0])
    k = k_ref[0]
    key_at = lax.broadcasted_iota(jnp.int32, (k.shape[0], 1), 0)
    scores = dot(k, q * SCALE, 1, 1) + jnp.where(key_at < length, 0.0, NEG)
    e = jnp.exp(scores - jnp.max(scores, axis=0, keepdims=True))
    p = e / jnp.sum(e, axis=0, keepdims=True)
    dv_ref[0] = dot(p.astype(BF16), g, 1, 0).astype(BF16)
    dp = dot(v_ref[0], g, 1, 1)
    ds = p * (dp - jnp.sum(dp * p, axis=0, keepdims=True))
    ds = (ds * SCALE).astype(BF16)
    dk_ref[0] = dot(ds, q, 1, 0).astype(BF16)
    dq_ref[0] = merge(dot(ds, k, 0, 0)).astype(BF16)


def attend_back(lengths, q, k, v, g):
    n, rows, width = q.shape
    keys = k.shape[1]
    q_spec = pl.BlockSpec((1, rows, PAIR), lambda s, h, l: (s, 0, h))
    k_spec = pl.BlockSpec((1, keys, PAIR), lambda s, h, l: (s, 0, h))
    return pl.pallas_call(
        attend_back_kernel,
        grid_spec=pltpu.PrefetchScalarGridSpec(
            num_scalar_prefetch=1,
            grid=(n, width // PAIR),
            in_specs=[q_spec, k_spec, k_spec, q_spec],
            out_specs=[q_spec, k_spec, k_spec],
        ),
        out_shape=[
            jax.ShapeDtypeStruct(q.shape, BF16),
            jax.ShapeDtypeStruct(k.shape, BF16),
            jax.ShapeDtypeStruct(k.shape, BF16),
        ],
        cost_estimate=pl.CostEstimate(
            flops=10 * n * rows * keys * width * 4, bytes_accessed=4 * n * (rows + 2 * keys) * width,
            transcendentals=n * rows * keys * width // HD,
        ),
        name="attend_back",
    )(lengths, q, k, v, g)


def norm_parts(y):
    centered = y - jnp.mean(y, axis=-1, keepdims=True)
    rstd = lax.rsqrt(jnp.mean(centered * centered, axis=-1, keepdims=True) + EPS)
    return centered * rstd, rstd


def norm_back(grad, gain, hat, rstd):
    scaled = grad * gain
    return rstd * (
        scaled
        - jnp.mean(scaled, axis=-1, keepdims=True)
        - hat * jnp.mean(scaled * hat, axis=-1, keepdims=True)
    )


def mm(a, b):
    return jnp.dot(a, b, preferred_element_type=F32)


def mm_nt(a, b):
    return lax.dot_general(a, b, (((1,), (1,)), ((), ())), preferred_element_type=F32)


def mm_tn(a, b):
    return lax.dot_general(a, b, (((0,), (0,)), ((), ())), preferred_element_type=F32)


def reduce_steps(chunks, ins, outs, acc_ref, halves_ref, quarter_ref, eighth_ref, send_sem, recv_sem):
    w, z = lax.axis_index("dp"), lax.axis_index("tensor")
    bit = {"c": lax.rem(w, 2), "x": lax.rem(w // 2, 2), "y": lax.rem(w // 4, 2)}
    peer = {"c": flip(w, 1), "x": flip(w, 2), "y": flip(w, 4)}
    barrier = pltpu.get_barrier_semaphore()
    for p in peer.values():
        pl.semaphore_signal(barrier, inc=1, device_id={"dp": p, "tensor": z}, device_id_type=MESH_ID)
    pl.semaphore_wait(barrier, 3)
    before = [sum(n for _, _, n in chunks[:c]) for c in range(len(chunks))]
    streams = (("x", "y"), ("y", "x"))

    def at(ref, start, n):
        return ref.at[pl.ds(pl.multiple_of(start, 8), n)]

    def places(c):
        r, o, n = chunks[c]
        h = before[c] // 2
        mine = o + bit["c"] * (n // 2)
        inner = [i * (n // 4) + bit[p] * (n // 8) for i, (p, _) in enumerate(streams)]
        other = [i * (n // 4) + (1 - bit[p]) * (n // 8) for i, (p, _) in enumerate(streams)]
        return ins[r], outs[r], o, n, h, mine, inner, other

    def copy(c, j):
        x, out, o, n, h, mine, inner, other = places(c)
        i = (j - 1) % 2
        p, p2 = streams[i]
        e, f = n // 8, n // 16
        kept = inner[i] + bit[p2] * f
        if j == 0:
            axis, src, dst = "c", at(x, o + (1 - bit["c"]) * (n // 2), n // 2), halves_ref.at[pl.ds(h, n // 2)]
        elif j < 3:
            axis, src, dst = p, at(acc_ref, h + other[i], e), quarter_ref.at[pl.ds(h // 2 + i * e, e)]
        elif j < 5:
            axis, src, dst = p2, at(acc_ref, h + inner[i] + (1 - bit[p2]) * f, f), eighth_ref.at[pl.ds(h // 4 + i * f, f)]
        elif j < 7:
            axis, src, dst = p2, at(out, mine + kept, f), at(out, mine + kept, f)
        elif j < 9:
            axis, src, dst = p, at(out, mine + inner[i], e), at(out, mine + inner[i], e)
        else:
            axis, src, dst = "c", at(out, mine, n // 2), at(out, mine, n // 2)
        return pltpu.make_async_remote_copy(
            src_ref=src, dst_ref=dst, send_sem=send_sem.at[c, j], recv_sem=recv_sem.at[c, j],
            device_id={"dp": peer[axis], "tensor": z}, device_id_type=MESH_ID,
        )

    def add(dst, d_at, a, a_at, b, b_at, n):
        size = 16 if n % 16 == 0 else 8
        rows = lambda start, k: pl.ds(pl.multiple_of(start + k * size, 8), size)

        def one(k, carry):
            dst[rows(d_at, k)] = a[rows(a_at, k)] + b[rows(b_at, k)]
            return carry

        lax.fori_loop(0, n // size, one, 0)

    def stage(c, s):
        x, out, o, n, h, mine, inner, other = places(c)
        e, f = n // 8, n // 16
        if s == 0:
            copy(c, 0).start()
        elif s == 1:
            copy(c, 0).wait_recv()
            add(acc_ref, h, x, mine, halves_ref, h, n // 2)
            for i in range(2):
                copy(c, 1 + i).start()
        elif s == 2:
            for i in range(2):
                copy(c, 1 + i).wait_recv()
                add(acc_ref, h + inner[i], acc_ref, h + inner[i], quarter_ref, h // 2 + i * e, e)
                copy(c, 3 + i).start()
        elif s == 3:
            for i, (_, p2) in enumerate(streams):
                copy(c, 3 + i).wait_recv()
                kept = inner[i] + bit[p2] * f
                add(out, mine + kept, acc_ref, h + kept, eighth_ref, h // 4 + i * f, f)
                copy(c, 5 + i).start()
        elif s == 4:
            for i in range(2):
                copy(c, 5 + i).wait_recv()
                copy(c, 7 + i).start()
        elif s == 5:
            for i in range(2):
                copy(c, 7 + i).wait_recv()
            copy(c, 9).start()
        else:
            copy(c, 9).wait_recv()

    def tick(t):
        for s in range(7):
            if 0 <= t - s < len(chunks):
                stage(t - s, s)

    def finish():
        for c in range(len(chunks)):
            for j in range(10):
                copy(c, j).wait_send()

    return len(chunks) + 6, tick, finish


def gelu_cdf(x):
    return 0.5 * (1.0 + lax.erf(x * 0.7071067811865476))


def last_kernel(chunks, n_in, *refs):
    ins, rest = refs[:n_in], refs[n_in:]
    tok_hbm, att_hbm, out_hbm, up_hbm, down_hbm, vec_ref, bup_ref = rest[:7]
    outs, y_ref = rest[7 : 7 + n_in], rest[7 + n_in]
    tok_ref, att_ref, wout_ref, up_ref, down_ref, norm_ref, low_ref, sum_ref, load_sem = rest[8 + n_in : 17 + n_in]
    loads = [
        pltpu.make_async_copy(src, dst, load_sem.at[i])
        for i, (src, dst) in enumerate((
            (tok_hbm, tok_ref), (att_hbm, att_ref), (out_hbm, wout_ref), (up_hbm, up_ref), (down_hbm, down_ref),
        ))
    ]
    for load in loads:
        load.start()
    ticks, tick, finish = reduce_steps(chunks, ins, outs, *rest[17 + n_in :])
    tick(0)
    for load in loads:
        load.wait()
    b_out, gain1, bias1, b_down, gain2, bias2 = (vec_ref[i : i + 1] for i in range(6))
    tile, block = norm_ref.shape[0], bup_ref.shape[1]
    blocks = bup_ref.shape[0]
    total = tok_ref.shape[0] // tile * blocks
    due = [1 + (j * total * PACE) // (8 * ticks - 8) for j in range(ticks - 1)]

    def compute(t, carry):
        for j in range(1, ticks):
            @pl.when(t == due[j - 1] - 1)
            def _():
                tick(j)

        at = pl.ds(pl.multiple_of(t // blocks * tile, tile), tile)
        b = lax.rem(t, blocks)

        @pl.when(b == 0)
        def _():
            hat, _ = norm_parts(tok_ref[at].astype(F32) + dot(att_ref[at], wout_ref[...], 1, 0) + b_out)
            normed = hat * gain1 + bias1
            norm_ref[...] = normed
            low_ref[...] = normed.astype(BF16)
            sum_ref[...] = normed + b_down

        units = pl.ds(pl.multiple_of(b * block, block), block)
        inner = dot(low_ref[...], up_ref[units], 1, 1) + bup_ref[pl.ds(b, 1)]
        active = (inner * gelu_cdf(inner)).astype(BF16)
        sum_ref[...] += dot(active, down_ref[units], 1, 0)

        @pl.when(b == blocks - 1)
        def _():
            hat, _ = norm_parts(sum_ref[...])
            y_ref[at] = (hat * gain2 + bias2).astype(BF16)

        return carry

    lax.fori_loop(0, total, compute, 0)
    finish()


def last(outer, arrays, step, cid, tok, att, w_out, up, down, vectors, b_up, tile, block):
    chunks = []
    for r, a in enumerate(arrays):
        for o in range(0, a.shape[0], step):
            chunks.append((r, o, min(step, a.shape[0] - o)))
    total = sum(n for _, _, n in chunks)
    width = tok.shape[1]
    vmem = lambda rows, dtype: pltpu.VMEM((rows, width), dtype)
    dma = pltpu.SemaphoreType.DMA
    spec = pl.BlockSpec(memory_space=pltpu.VMEM)
    big = (tok, att, w_out, up, down)
    *sums, y = pl.pallas_call(
        functools.partial(last_kernel, tuple(chunks), len(arrays)),
        out_shape=[jax.ShapeDtypeStruct(a.shape, F32) for a in arrays] + [jax.ShapeDtypeStruct(tok.shape, BF16)],
        in_specs=[spec] * len(arrays) + [pl.BlockSpec(memory_space=pl.ANY)] * 5 + [spec] * 2,
        out_specs=[spec] * (len(arrays) + 1),
        scratch_shapes=[vmem(a.shape[0], BF16) for a in big] + [
            vmem(tile, F32), vmem(tile, BF16), vmem(tile, F32), dma((5,)),
            vmem(total // 2, F32), vmem(total // 2, F32), vmem(total // 4, F32), vmem(total // 8, F32),
            dma((len(chunks), 10)), dma((len(chunks), 10)),
        ],
        compiler_params=pltpu.CompilerParams(collective_id=cid, has_side_effects=True, vmem_limit_bytes=VMEM_LAST),
        name="last",
    )(*arrays, *big, vectors, b_up.reshape(-1, block))
    if outer is not None:
        sums = [lax.psum(a, "dp", axis_index_groups=outer) for a in sums]
    return sums, y


def my_share(which, p):
    return lax.dynamic_index_in_dim(
        p.reshape(GROUP, p.shape[0] // GROUP, p.shape[1]), lax.rem(which, GROUP), 0, keepdims=False
    )


def body(
    ranks, outer, tokens, w_qkv, b_qv, w_out, b_out, ln1_gain, ln1_bias, w_up, b_up, w_down, b_down,
    ln2_gain, ln2_bias, lengths, picks, cotangent,
):
    rank = lax.axis_index("tensor")
    which = lax.axis_index("dp")
    seqs = lengths.shape[0]
    rows, width = tokens.shape
    seq = rows // seqs
    slots = picks.shape[1]
    part = w_qkv.shape[2]
    hidden = w_up.shape[1]

    by_seq = tokens.reshape(seqs, seq, width)
    chosen = (picks[:, :, None] == jnp.arange(seq)[None, None, :])
    chosen_low = chosen.astype(BF16)
    chosen_f32 = chosen.astype(F32)
    picked = jnp.einsum("spk,skd->spd", chosen_low, by_seq, preferred_element_type=F32).astype(BF16)
    picked_rows = picked.reshape(seqs * slots, width)

    own_qkv = jnp.swapaxes(w_qkv, 1, 2).reshape(3 * part, width)
    head = my_share(which, own_qkv).astype(F32)
    parts = (w_out, w_up.T, w_down)
    shares = [my_share(which, p).astype(F32) for p in parts]
    spots = lax.dynamic_update_slice_in_dim(jnp.zeros((2, width), F32), b_qv, rank * part, 1)
    vectors = jnp.concatenate([b_up.reshape(1, width), spots, jnp.zeros((5, width), F32)], axis=0)
    keys, values, q_picked, attended, _, all_vectors, all_qkv, all_out, all_up, all_down = front(
        ranks, SPACE, by_seq, picked, own_qkv, lengths, head, parts, shares, vectors
    )
    all_b_up = all_vectors[:, 0].reshape(-1)
    att_picked = jnp.einsum("spk,skd->spd", chosen_low, attended, preferred_element_type=F32).astype(BF16)
    grad_output = jnp.einsum(
        "spk,skd->spd", chosen_f32, cotangent.reshape(seqs, seq, width),
        precision=lax.Precision.HIGH, preferred_element_type=F32,
    ).reshape(seqs * slots, width)
    def forward(tok, att):
        first_sum = tok.astype(F32) + mm(att, all_out) + b_out
        hat1, rstd1 = norm_parts(first_sum)
        normed = hat1 * ln1_gain + ln1_bias
        normed_low = normed.astype(BF16)
        inner = mm_nt(normed_low, all_up) + all_b_up
        cdf = gelu_cdf(inner)
        active = (inner * cdf).astype(BF16)
        hat2, rstd2 = norm_parts(normed + mm(active, all_down) + b_down)
        return hat1, rstd1, normed_low, inner, cdf, active, hat2, rstd2

    att = att_picked.reshape(-1, width)
    hat1, rstd1, normed_low, inner, cdf, active, hat2, rstd2 = forward(picked_rows, att)
    grad_second = norm_back(grad_output, ln2_gain, hat2, rstd2)
    g_ln2_gain = jnp.sum(grad_output * hat2, axis=0)
    g_ln2_bias = jnp.sum(grad_output, axis=0)
    g_b_down = jnp.sum(grad_second, axis=0)
    second_low = grad_second.astype(BF16)
    own_hidden = lambda x: lax.dynamic_slice_in_dim(x, rank * hidden, hidden, 1)
    own_part = lambda x: lax.dynamic_slice_in_dim(x, rank * part, part, x.ndim - 1)
    g_w_down = mm_tn(own_hidden(active), second_low)
    grad_active = mm_nt(second_low, all_down)
    slope = cdf + inner * (0.3989422804014327 * jnp.exp(-0.5 * inner * inner))
    grad_inner = (grad_active * slope).astype(BF16)
    own_inner = own_hidden(grad_inner)
    g_b_up = jnp.sum(own_inner, axis=0, dtype=F32)
    g_w_up = mm_tn(normed_low, own_inner)
    grad_normed = grad_second + mm(grad_inner, all_up)
    grad_first = norm_back(grad_normed, ln1_gain, hat1, rstd1)
    g_ln1_gain = jnp.sum(grad_normed * hat1, axis=0)
    g_ln1_bias = jnp.sum(grad_normed, axis=0)
    g_b_out = jnp.sum(grad_first, axis=0)
    first_low = grad_first.astype(BF16)
    g_w_out = mm_tn(own_part(att), first_low)
    grad_att = mm_nt(first_low, all_out).astype(BF16)
    dq, dk, dv = attend_back(lengths, q_picked, keys, values, grad_att.reshape(seqs, slots, width))
    dq_rows = dq.reshape(seqs * slots, width)
    dk_rows = dk.reshape(rows, width)
    dv_rows = dv.reshape(rows, width)
    own_q, own_k, own_v = own_part(dq_rows), own_part(dk_rows), own_part(dv_rows)
    g_b_qv = jnp.concatenate([jnp.sum(own_q, axis=0, dtype=F32), jnp.sum(own_v, axis=0, dtype=F32)])
    g_vectors = jnp.concatenate([
        g_b_out, g_ln1_gain, g_ln1_bias, g_b_down, g_ln2_gain, g_ln2_bias, g_b_up, g_b_qv,
        jnp.zeros((8 * width - 6 * width - hidden - 2 * part,), F32),
    ]).reshape(8, width)
    used_rows = part + 3 * part + 8
    g_last = jnp.concatenate([
        g_w_out, mm_tn(own_q, picked_rows), mm_tn(own_k, tokens), mm_tn(own_v, tokens), g_vectors,
        jnp.zeros((-used_rows % 128, width), F32),
    ], axis=0)
    vectors = jnp.stack([b_out, ln1_gain, ln1_bias, b_down, ln2_gain, ln2_bias, b_out, b_out])
    (g_w_down, g_w_up, g_last), output = last(
        outer, [g_w_down, g_w_up, g_last], 384, 2, tokens, attended.reshape(rows, width), all_out, all_up, all_down,
        vectors, all_b_up, 512, 384,
    )
    g_w_out, g_last = g_last[:part], g_last[part:]
    sparse = (grad_first + mm(dq_rows, all_qkv[0])).reshape(seqs, slots, width)
    grad_tokens = (
        jnp.einsum("spk,spd->skd", chosen_f32, sparse, precision=lax.Precision.HIGH,
                   preferred_element_type=F32).reshape(rows, width)
        + mm(dk_rows, all_qkv[1])
        + mm(dv_rows, all_qkv[2])
    )
    g_w_qkv = jnp.swapaxes(g_last[: 3 * part].reshape(3, part, width), 1, 2)
    g_vectors = g_last[3 * part :].reshape(-1)
    g_b_out, g_ln1_gain, g_ln1_bias, g_b_down, g_ln2_gain, g_ln2_bias = (
        g_vectors[i * width : (i + 1) * width] for i in range(6)
    )
    g_b_up = g_vectors[6 * width : 6 * width + hidden]
    g_b_qv = g_vectors[6 * width + hidden : 6 * width + hidden + 2 * part].reshape(2, part)
    return (
        output, grad_tokens, g_w_qkv, g_b_qv, g_w_out, g_b_out, g_ln1_gain, g_ln1_bias, g_w_up, g_b_up,
        g_w_down, g_b_down, g_ln2_gain, g_ln2_bias,
    )


def solution(mesh):
    in_specs = (
        P("dp", None), P(None, None, "tensor"), P(None, "tensor"), P("tensor", None), P(), P(), P(),
        P(None, "tensor"), P("tensor"), P("tensor", None), P(), P(), P(), P("dp"), P("dp", None), P("dp", None),
    )
    out_specs = (
        P("dp", None), P("dp", None), P(None, None, "tensor"), P(None, "tensor"), P("tensor", None), P(), P(),
        P(), P(None, "tensor"), P("tensor"), P("tensor", None), P(), P(), P(),
    )
    ranks, copies = mesh.shape["tensor"], mesh.shape["dp"]
    outer = None
    if copies > GROUP:
        outer = [[g + j for g in range(0, copies, GROUP)] for j in range(GROUP)]
    step = functools.partial(body, ranks, outer)
    return jax.shard_map(step, mesh=mesh, in_specs=in_specs, out_specs=out_specs, check_vma=False)
```
